256 devices in a mesh: atoms: 32 (over z, x), bands: 8 (over y, core).
Axes of the slice: x: 4, y: 4, z: 8, core: 2. Of those that a mesh axis runs over, the one named last changes fastest.
Arguments:
- eigvecs: bfloat16 [32768, 8192], P('atoms', 'bands'), may hold values from -0.59765625 to 0.59765625
- occupations: float32 [8192], P('bands'), may hold values from 0.2 to 2
- energies: float32 [8192], P('bands'), may hold values from -1 to 0.5
- neighbours: int32 [256, 16], P('atoms'), may hold values from 0 to 255, as said below
Outputs:
- density: float32 [256, 16, 128, 128], P('atoms', None, 'bands')
- energy_density: float32 [256, 16, 128, 128], P('atoms', None, 'bands')
The draws below stay inside these ranges and needn't reach their ends.
Inputs may be any that keep to these rules, and one draw needn't show every extreme that they name: `neighbours`: every block named in the rows of one atoms domain lies in that domain or in one of the 2 domains on either side along the atoms axis, taken cyclically; from each of those 4 other domains the rows of one domain name exactly 2 distinct blocks.
All inputs are finite; a program needn't handle non-finite values.
Results may differ from the reference program's by a relative error of at most 0.014.
Values may be sent and summed in bfloat16 or wider, within the bound.
A program may use at most 128 MiB of HBM per device.

```python
import jax
import jax.numpy as jnp
from jax import lax

NB_DEV = 8
K = 16
CAP = 2
R = 2
TILE = 128
NBAND = 8192
NB = 256
ORBITALS = 32768
N_BANDS = 8


def draw_neighbours(key, part):
    domain_count = NB // NB_DEV
    pool_size = NB_DEV + 2 * R * CAP
    total_slots = NB_DEV * K

    def one_domain(domain_key, domain):
        keys = jax.random.split(domain_key, 2 * R + 2)
        pools = [domain * NB_DEV + jnp.arange(NB_DEV, dtype=jnp.int32)]
        offsets = list(range(-R, 0)) + list(range(1, R + 1))
        for place, offset in enumerate(offsets):
            peer = (domain + offset) % domain_count
            picked = jax.random.permutation(keys[place], NB_DEV)[:CAP].astype(jnp.int32)
            pools.append(peer * NB_DEV + picked)
        pool = jnp.concatenate(pools, 0)
        extra = jax.random.randint(keys[2 * R], (total_slots,), 0, pool_size)
        slots = jnp.arange(total_slots, dtype=jnp.int32)
        which = jnp.where(slots < pool_size, slots, extra)
        values = pool[which]
        order = jax.random.permutation(keys[2 * R + 1], total_slots)
        return values[order].reshape(NB_DEV, K)
    domain_keys = jax.random.split(key, domain_count)
    result = jax.vmap(one_domain)(domain_keys, jnp.arange(domain_count, dtype=jnp.int32))
    return result.reshape(NB, K).astype(jnp.int32)


def levels(rng, shape, cuts, smallest, top_value):
    def one(position, shards_of):
        heights = jax.random.uniform(jax.random.fold_in(jax.random.fold_in(rng, 6), position), (shards_of,), jnp.float32, smallest / len(cuts), top_value / len(cuts))
        return jnp.repeat(jnp.exp(heights), shape[position] // shards_of).reshape((-1,) + (1,) * (len(shape) - position - 1))

    factor_of = one(*cuts[0])
    for cut in cuts[1:]:
        factor_of = factor_of * one(*cut)
    return factor_of


def scatter_about(stream_key, extent, width, most, pieces=(), kind=jnp.bfloat16):
    drawn = jax.random.normal(stream_key, extent, jnp.float32) * width
    if len(pieces) > 0:
        drawn = levels(stream_key, extent, pieces, -0.22, 0.18) * drawn
    return jnp.clip(drawn, min=-most, max=most).astype(kind)


def setup_inputs(seed: int = 0) -> dict:
    key_of = jax.random.split(jax.random.key(seed), 5)
    return {
        "eigvecs": scatter_about(key_of[0], (ORBITALS, NBAND), 0.1, 0.59765625, ((0, 32), (1, 8))),
        "occupations": jnp.clip(0.2 + 1.8 * jax.random.uniform(key_of[1], (NBAND,), jnp.float32) ** levels(key_of[1], (NBAND,), ((0, 8),), -0.2, 0.2), 0.2, 2.0),
        "energies": jnp.clip(-1.0 + 1.5 * jax.random.uniform(key_of[2], (NBAND,), jnp.float32) ** levels(key_of[2], (NBAND,), ((0, 8),), -0.2, 0.2), -1.0, 0.5),
        "neighbours": draw_neighbours(jax.random.fold_in(key_of[4], 71), 0),
    }


def reference(eigvecs, occupations, energies, neighbours):
    rows = eigvecs.reshape(NB, TILE, N_BANDS, NBAND // N_BANDS)
    occ_groups = occupations.reshape(N_BANDS, NBAND // N_BANDS)
    weight_groups = (occupations * energies).reshape(N_BANDS, NBAND // N_BANDS)
    scaled_p = (rows.astype(jnp.float32) * occ_groups).astype(jnp.bfloat16)
    scaled_w = (rows.astype(jnp.float32) * weight_groups).astype(jnp.bfloat16)
    scaled = jnp.stack([scaled_p, scaled_w], 1)

    def one_block(pair):
        left, block_ids = pair
        right = rows[block_ids.astype(jnp.int32)].astype(jnp.float32)
        part = jnp.einsum("sagb,kcgb->gksac", left.astype(jnp.float32), right)
        part = lax.optimization_barrier(part.astype(jnp.bfloat16))
        return jnp.sum(part.astype(jnp.float32), axis=0)

    tiles = lax.map(one_block, (scaled, neighbours))
    return tiles[:, :, 0], tiles[:, :, 1]
```

```python
import functools

import jax
import jax.numpy as jnp
from jax import lax
from jax.experimental import pallas as pl
from jax.experimental.pallas import tpu as pltpu
from jax.sharding import PartitionSpec as P

F32 = jnp.float32
BF16 = jnp.bfloat16
MESH = pl.DeviceIdType.MESH
CORES = 2
PAIR = 2


def exchange_kernel(
    eig, occ, en, neigh,
    tiles_out, pos_out,
    own, mate, far, lhs, vec, ybuf, r1, fbuf, gbuf, s2, send, relay, req_out, req_in, neigh_v, pos_v, tiles,
    ld_sem, own_send, own_recv, vec_send, vec_recv, req_send, req_recv,
    x_send, x_recv, fwd_send, fwd_recv, y_send, y_recv, out_sem,
):
    n = lax.axis_size("atoms")
    d = lax.axis_index("atoms")
    band = lax.axis_index("bands")
    bands = lax.axis_size("bands")
    ny = bands // CORES
    y = band // CORES
    c = lax.rem(band, CORES)
    blocks = neigh.shape[0]
    tile = eig.shape[1]
    keep = tile // bands
    stages = ybuf.shape[0]
    own_stages = blocks // PAIR
    wide = PAIR * tile
    group = blocks * keep

    def at_domain(step):
        return (lax.rem(d + step + n, n), band)

    def at_y(step):
        return (d, lax.rem(y + step + ny, ny) * CORES + c)

    partner = (d, y * CORES + 1 - c)
    x_to = (at_domain(1), at_domain(-1))
    y_to = (at_y(1), at_y(-1))
    peers = [at_domain(s) for s in (1, -1, 2, -2)] + [y_to[0], y_to[1], partner]

    barrier = pltpu.get_barrier_semaphore()
    for peer in peers:
        pl.semaphore_signal(barrier, inc=1, device_id=peer, device_id_type=MESH)

    load_ids = pltpu.make_async_copy(neigh, neigh_v, ld_sem.at[0])
    load_occ = pltpu.make_async_copy(occ, vec.at[0, 0], ld_sem.at[1])
    load_en = pltpu.make_async_copy(en, vec.at[0, 1], ld_sem.at[2])
    load_eig = pltpu.make_async_copy(eig, own, ld_sem.at[3])
    load_ids.start()
    load_occ.start()
    load_en.start()
    load_eig.start()

    load_ids.wait()
    ids = neigh_v[...]
    shift = blocks.bit_length() - 1
    owner = lax.shift_right_logical(ids, jnp.full_like(ids, shift))
    within = ids & (blocks - 1)
    pos = within
    row = lax.broadcasted_iota(jnp.int32, req_out.shape[1:], 0)
    steps = (-1, 1, -2, 2)
    for q, step in enumerate(steps):
        mask = owner == lax.rem(d + step + n, n)
        low = jnp.min(jnp.where(mask, within, blocks - 1))
        high = jnp.max(jnp.where(mask, within, 0))
        req_out[q] = jnp.where(row == 0, low, high)
        base = blocks + 4 * (q // 2) + q % 2
        pos = jnp.where(mask, base + 2 * (within != low).astype(jnp.int32), pos)
    pos_v[...] = pos
    put_pos = pltpu.make_async_copy(pos_v, pos_out, out_sem.at[stages])
    put_pos.start()

    def remote(src, dst, s_sem, r_sem, to):
        return pltpu.make_async_remote_copy(
            src_ref=src, dst_ref=dst, send_sem=s_sem, recv_sem=r_sem,
            device_id=to, device_id_type=MESH,
        )

    pl.semaphore_wait(barrier, len(peers))

    asks = [
        remote(req_out.at[q], req_in.at[q], req_send.at[q], req_recv.at[q], at_domain(step))
        for q, step in enumerate(steps)
    ]
    for ask in asks:
        ask.start()
    swaps = [
        remote(occ, vec.at[1, 0], vec_send.at[0], vec_recv.at[0], partner),
        remote(en, vec.at[1, 1], vec_send.at[1], vec_recv.at[1], partner),
    ]
    for s in range(own_stages):
        rows = pl.ds(s * PAIR, PAIR)
        swaps.append(
            remote(eig.at[rows], mate.at[rows], own_send.at[s], own_recv.at[s], partner)
        )
    for swap in swaps:
        swap.start()

    def scale(kc, source):
        first = vec[kc, 0]
        second = first * vec[kc, 1]

        def step(t, carry):
            rel = t // blocks
            i = lax.rem(t, blocks)
            dest = lax.rem(y + rel, ny)
            at = pl.multiple_of((dest * CORES + c) * keep, keep)
            x = source[i, pl.ds(at, keep), :].astype(F32)
            to = pl.multiple_of(rel * 2 * group + i * keep, keep)
            lhs[kc, pl.ds(to, keep), :] = (x * first).astype(BF16)
            to = pl.multiple_of(rel * 2 * group + group + i * keep, keep)
            lhs[kc, pl.ds(to, keep), :] = (x * second).astype(BF16)
            return carry

        lax.fori_loop(0, ny * blocks, step, 0)

    load_occ.wait()
    load_en.wait()
    load_eig.wait()
    scale(0, own)

    for ask in asks:
        ask.wait_recv()
    hops = {}
    for rank in range(2):
        for side in range(2):
            for kind in range(2):
                q = 2 * kind + side
                b = jnp.max(req_in[q, rank:rank + 1, :])
                send[2 * q + rank] = own[b]
    for rank in range(2):
        for kind in range(2):
            for side in range(2):
                q = 2 * kind + side
                dst = far.at[0, 2 * rank + side] if kind == 0 else relay.at[2 * rank + side]
                hop = remote(
                    send.at[2 * q + rank], dst,
                    x_send.at[kind, rank, side], x_recv.at[kind, rank, side], x_to[side],
                )
                hop.start()
                hops[kind, rank, side] = hop

    for swap in swaps:
        swap.wait_recv()
    scale(1, mate)

    def multiply(s):
        if s < own_stages:
            right = [blk[pl.ds(s * PAIR, PAIR)].reshape(wide, -1) for blk in (own, mate)]
        else:
            right = [far[k, pl.ds((s - own_stages) * PAIR, PAIR)].reshape(wide, -1) for k in range(CORES)]
        half = lhs.shape[1] // 2
        dims = (((1,), (1,)), ((), ()))

        def step(m, carry):
            rows = pl.ds(pl.multiple_of(m * half, half), half)
            total = lax.dot_general(lhs[0, rows, :], right[0], dims, preferred_element_type=F32)
            total += lax.dot_general(lhs[1, rows, :], right[1], dims, preferred_element_type=F32)
            ybuf[s, rows, :] = total.astype(BF16)
            return carry

        lax.fori_loop(0, 2, step, 0)

    def piece(s, rel, which):
        return ybuf.at[s, pl.ds((2 * rel + which) * group, group), :]

    y_hops = {}

    def first_sends(s):
        plan = (
            (piece(s, 2, 0), r1.at[s, 0], 0),
            (piece(s, 2, 1), r1.at[s, 1], 1),
            (piece(s, 1, 1), fbuf.at[s, 1], 0),
            (piece(s, 3, 0), fbuf.at[s, 0], 1),
        )
        for k, (src, dst, side) in enumerate(plan):
            y_hops[s, k] = remote(src, dst, y_send.at[s, k], y_recv.at[s, k], y_to[side])
            y_hops[s, k].start()

    def second_sends(s):
        for which in range(2):
            y_hops[s, which].wait_recv()
            rel = 1 if which == 0 else 3
            s2[s, which] = (r1[s, which].astype(F32) + piece(s, rel, which)[...].astype(F32)).astype(BF16)
            y_hops[s, 4 + which] = remote(
                s2.at[s, which], gbuf.at[s, which], y_send.at[s, 4 + which], y_recv.at[s, 4 + which], y_to[which],
            )
            y_hops[s, 4 + which].start()

    puts = []

    def finish(s):
        for k in (2, 3, 4, 5):
            y_hops[s, k].wait_recv()
        for which in range(2):
            total = piece(s, 0, which)[...].astype(F32) + fbuf[s, which].astype(F32) + gbuf[s, which].astype(F32)
            for jj in range(PAIR):
                tiles[which, PAIR * s + jj] = total[:, jj * tile:(jj + 1) * tile]
        blk = pl.ds(PAIR * s, PAIR)
        put = pltpu.make_async_copy(tiles.at[:, blk], tiles_out.at[:, blk], out_sem.at[s])
        put.start()
        puts.append(put)

    forwards = {}

    def forward(kind, rank):
        for side in range(2):
            hops[kind, rank, side].wait_recv()
            k = 2 * kind + 2 * rank + side
            forwards[k] = remote(
                far.at[0, k], far.at[1, k], fwd_send.at[k], fwd_recv.at[k], partner
            )
            forwards[k].start()

    def pass_on(rank):
        for side in range(2):
            hops[1, rank, side].wait_recv()
            hop = remote(
                relay.at[2 * rank + side], far.at[0, 4 + 2 * rank + side],
                x_send.at[2, rank, side], x_recv.at[2, rank, side], x_to[side],
            )
            hop.start()
            hops[2, rank, side] = hop

    def remote_stage(s):
        for side in range(2):
            forwards[PAIR * (s - own_stages) + side].wait_recv()
        multiply(s)
        first_sends(s)

    for s in range(own_stages):
        multiply(s)
        first_sends(s)
    second_sends(0)
    forward(0, 0)
    second_sends(1)
    remote_stage(4)
    second_sends(2)
    pass_on(0)
    second_sends(3)
    forward(0, 1)
    second_sends(4)
    remote_stage(5)
    finish(0)
    finish(1)
    finish(2)
    pass_on(1)
    finish(3)
    finish(4)
    second_sends(5)
    forward(2, 0)
    remote_stage(6)
    finish(5)
    second_sends(6)
    forward(2, 1)
    remote_stage(7)
    finish(6)
    second_sends(7)
    finish(7)

    for copy in asks + swaps + list(hops.values()) + list(forwards.values()) + list(y_hops.values()):
        copy.wait_send()
    put_pos.wait()
    for put in puts:
        put.wait()


def place_kernel(pos, tiles, density, energy):
    per, slots = density.shape[:2]
    first = pl.program_id(0) * per
    for i in range(per):
        for k in range(slots):
            p = pos[first + i, k]
            density[i, k] = tiles[0, p, i]
            energy[i, k] = tiles[1, p, i]


def body(eigvecs, occupations, energies, neighbours):
    bands = lax.axis_size("bands")
    blocks, slots = neighbours.shape
    rows, depth = eigvecs.shape
    tile = rows // blocks
    keep = tile // bands
    group = blocks * keep
    ny = bands // CORES
    pool_blocks = blocks + 8
    stages = pool_blocks // PAIR
    wide = PAIR * tile
    any_space = pl.BlockSpec(memory_space=pl.ANY)
    dma = pltpu.SemaphoreType.DMA
    tiles, pos = pl.pallas_call(
        exchange_kernel,
        out_shape=(
            jax.ShapeDtypeStruct((2, pool_blocks, group, tile), F32),
            jax.ShapeDtypeStruct((blocks, slots), jnp.int32),
        ),
        in_specs=[any_space] * 4,
        out_specs=(any_space, any_space),
        scratch_shapes=[
            pltpu.VMEM((blocks, tile, depth), BF16),
            pltpu.VMEM((blocks, tile, depth), BF16),
            pltpu.VMEM((CORES, 8, tile, depth), BF16),
            pltpu.VMEM((CORES, ny * 2 * group, depth), BF16),
            pltpu.VMEM((CORES, 2, 1, depth), F32),
            pltpu.VMEM((stages, ny * 2 * group, wide), BF16),
            pltpu.VMEM((stages, 2, group, wide), BF16),
            pltpu.VMEM((stages, 2, group, wide), BF16),
            pltpu.VMEM((stages, 2, group, wide), BF16),
            pltpu.VMEM((stages, 2, group, wide), BF16),
            pltpu.VMEM((8, tile, depth), BF16),
            pltpu.VMEM((4, tile, depth), BF16),
            pltpu.VMEM((4, 8, 128), jnp.int32),
            pltpu.VMEM((4, 8, 128), jnp.int32),
            pltpu.VMEM((blocks, slots), jnp.int32),
            pltpu.VMEM((blocks, slots), jnp.int32),
            pltpu.VMEM((2, pool_blocks, group, tile), F32),
            dma((4,)),
            dma((blocks // PAIR,)),
            dma((blocks // PAIR,)),
            dma((2,)),
            dma((2,)),
            dma((4,)),
            dma((4,)),
            dma((3, 2, 2)),
            dma((3, 2, 2)),
            dma((8,)),
            dma((8,)),
            dma((stages, 6)),
            dma((stages, 6)),
            dma((stages + 1,)),
        ],
        compiler_params=pltpu.CompilerParams(
            collective_id=0, has_side_effects=True, vmem_limit_bytes=60 * 2**20
        ),
        name="exchange",
    )(eigvecs.reshape(blocks, tile, depth), occupations.reshape(1, depth), energies.reshape(1, depth), neighbours)
    tiles = tiles.reshape(2, pool_blocks, blocks, keep, tile)
    per = 2
    out = jax.ShapeDtypeStruct((blocks, slots, keep, tile), F32)
    density, energy = pl.pallas_call(
        place_kernel,
        out_shape=(out, out),
        grid_spec=pltpu.PrefetchScalarGridSpec(
            num_scalar_prefetch=1,
            grid=(blocks // per,),
            in_specs=[pl.BlockSpec((2, pool_blocks, per, keep, tile), lambda i, pos: (0, 0, i, 0, 0))],
            out_specs=[pl.BlockSpec((per, slots, keep, tile), lambda i, pos: (i, 0, 0, 0))] * 2,
        ),
        name="place",
    )(pos, tiles)
    return density, energy


def solution(mesh):
    return jax.shard_map(
        body,
        mesh=mesh,
        in_specs=(P("atoms", "bands"), P("bands"), P("bands"), P("atoms", None)),
        out_specs=(P("atoms", None, "bands", None), P("atoms", None, "bands", None)),
        check_vma=False,
    )
```

```python
import jax
import jax.numpy as jnp
from jax import lax
from jax.experimental import pallas as pl
from jax.experimental.pallas import tpu as pltpu
from jax.sharding import PartitionSpec as P

F32 = jnp.float32
BF16 = jnp.bfloat16
MESH = pl.DeviceIdType.MESH
CORES = 2
PAIR = 2
WHOLE = 6
HALVES = 4
FAR = 8
ORDER = (2, 1, 3, 0)


def exchange_kernel(
    eig, occ, en, neigh,
    tiles, pos_out,
    own, mate, far, lhs, vec,
    y_whole, rx_whole, y_half, rx_half,
    send, relay, req_out, req_in, neigh_v, pos_v,
    ld_sem, own_send, own_recv, vec_send, vec_recv, req_send, req_recv,
    x_send, x_recv, b_send, b_recv, fc_send, fc_recv, fb_send, fb_recv,
    yw_send, yw_recv, yh_send, yh_recv, out_sem,
):
    n = lax.axis_size("atoms")
    d = lax.axis_index("atoms")
    band = lax.axis_index("bands")
    y = band // CORES
    c = lax.rem(band, CORES)
    blocks, ny, _, keep, depth = eig.shape
    group = blocks * keep
    tile = ny * CORES * keep
    own_stages = blocks // PAIR

    def at_domain(step):
        return (lax.rem(d + step + n, n), band)

    def at_y(step):
        return (d, lax.rem(y + step + ny, ny) * CORES + c)

    partner = (d, y * CORES + 1 - c)
    x_to = (at_domain(1), at_domain(-1))
    y_to = (at_y(1), at_y(-1))
    peers = [at_domain(s) for s in (2, -2, 1, -1)] + [y_to[0], y_to[1], partner]

    barrier = pltpu.get_barrier_semaphore()
    for peer in peers:
        pl.semaphore_signal(barrier, inc=1, device_id=peer, device_id_type=MESH)

    load_ids = pltpu.make_async_copy(neigh, neigh_v, ld_sem.at[0])
    load_occ = pltpu.make_async_copy(occ, vec.at[0, 0], ld_sem.at[1])
    load_en = pltpu.make_async_copy(en, vec.at[0, 1], ld_sem.at[2])
    load_eig = pltpu.make_async_copy(eig, own, ld_sem.at[3])
    load_ids.start()
    load_eig.start()
    load_occ.start()
    load_en.start()

    load_ids.wait()
    ids = neigh_v[...]
    shift = blocks.bit_length() - 1
    owner = lax.shift_right_logical(ids, jnp.full_like(ids, shift))
    within = ids & (blocks - 1)
    row = lax.broadcasted_iota(jnp.int32, req_out.shape[1:], 0)
    steps = (-1, 1, -2, 2)
    masks, lows = [], []
    for q, step in enumerate(steps):
        mask = owner == lax.rem(d + step + n, n)
        low = jnp.min(jnp.where(mask, within, blocks - 1))
        high = jnp.max(jnp.where(mask, within, 0))
        req_out[q] = jnp.where(row == 0, low, high)
        masks.append(mask)
        lows.append(low)

    def remote(src, dst, s_sem, r_sem, to):
        return pltpu.make_async_remote_copy(
            src_ref=src, dst_ref=dst, send_sem=s_sem, recv_sem=r_sem,
            device_id=to, device_id_type=MESH,
        )

    pl.semaphore_wait(barrier, len(peers))

    asks = [
        remote(req_out.at[q], req_in.at[q], req_send.at[q], req_recv.at[q], at_domain(step))
        for q, step in enumerate(steps)
    ]
    swaps = [
        remote(occ, vec.at[1, 0], vec_send.at[0], vec_recv.at[0], partner),
        remote(en, vec.at[1, 1], vec_send.at[1], vec_recv.at[1], partner),
        remote(eig.at[:, :, 1 - c], mate.at[:, :, 1 - c], own_send.at[own_stages], own_recv.at[own_stages], partner),
    ]
    for s in range(own_stages):
        blk = pl.ds(s * PAIR, PAIR)
        swaps.append(remote(eig.at[blk, :, c], mate.at[blk, :, c], own_send.at[s], own_recv.at[s], partner))
    for copy in asks + swaps:
        copy.start()

    pos = within
    for q in range(4):
        base = blocks + 4 * (q // 2) + q % 2
        pos = jnp.where(masks[q], base + 2 * (within != lows[q]).astype(jnp.int32), pos)
    pos_v[...] = pos
    put_pos = pltpu.make_async_copy(pos_v, pos_out, out_sem.at[0])
    put_pos.start()

    def scale(kc, source):
        first = vec[kc, 0]
        second = first * vec[kc, 1]
        for k, rel in enumerate(ORDER):
            dest = lax.rem(y + rel, ny)

            def step(i, carry, k=k, dest=dest):
                x = source[i, dest, c].astype(F32)
                at = pl.multiple_of(2 * k * group + i * keep, keep)
                lhs[kc, pl.ds(at, keep), :] = (x * first).astype(BF16)
                at = pl.multiple_of((2 * k + 1) * group + i * keep, keep)
                lhs[kc, pl.ds(at, keep), :] = (x * second).astype(BF16)
                return carry

            lax.fori_loop(0, blocks, step, 0)

    load_occ.wait()
    load_en.wait()
    load_eig.wait()
    scale(0, own)

    hops = {}
    for rank in range(2):
        for kind in range(2):
            for side in range(2):
                q = 2 * kind + side
                if rank == 0:
                    asks[q].wait_recv()
                b = jnp.max(req_in[q, rank:rank + 1, :])
                send[2 * q + rank] = own[b]
            for side in range(2):
                q = 2 * kind + side
                dst = far.at[0, 2 * rank + side] if kind == 0 else relay.at[2 * rank + side]
                hops[kind, rank, side] = remote(
                    send.at[2 * q + rank], dst,
                    x_send.at[kind, rank, side], x_recv.at[kind, rank, side], x_to[side],
                )
                hops[kind, rank, side].start()

    for swap in swaps[:3]:
        swap.wait_recv()
    scale(1, mate)

    y_hops = {}
    dims = (((1,), (1,)), ((), ()))

    class Stage:
        def __init__(self, s):
            self.s = s
            if s < WHOLE:
                self.out, self.rx = y_whole.at[s], rx_whole.at[s]
                self.y_send, self.y_recv = yw_send.at[s], yw_recv.at[s]
            else:
                self.out, self.rx = y_half.at[s - WHOLE], rx_half.at[s - WHOLE]
                self.y_send, self.y_recv = yh_send.at[s - WHOLE], yh_recv.at[s - WHOLE]

        def right(self, k):
            s = self.s
            if s < own_stages:
                value = (own, mate)[k][pl.ds(s * PAIR, PAIR)]
            elif s < WHOLE:
                value = far[k, pl.ds((s - own_stages) * PAIR, PAIR)]
            else:
                rank, half = (s - WHOLE) // 2, (s - WHOLE) % 2
                value = far[k, pl.ds(4 + 2 * rank, PAIR), pl.ds(half * (ny // 2), ny // 2)]
            return value.reshape(-1, depth)

        def piece(self, rel, which):
            return self.out.at[pl.ds((2 * ORDER.index(rel) + which) * group, group), :]

        def rows(self, first, count):
            rows = pl.ds(first * group, count * group)
            total = lax.dot_general(lhs[0, rows, :], self.right(0), dims, preferred_element_type=F32)
            total += lax.dot_general(lhs[1, rows, :], self.right(1), dims, preferred_element_type=F32)
            self.out[rows, :] = total.astype(BF16)

        def hop(self, k, src, side):
            copy = remote(src, self.rx.at[k], self.y_send.at[k], self.y_recv.at[k], y_to[side])
            copy.start()
            y_hops[self.s, k] = copy

        def run(self):
            self.rows(0, 2)
            self.hop(0, self.piece(2, 0), 0)
            self.hop(1, self.piece(2, 1), 1)
            self.rows(2, 4)
            self.hop(3, self.piece(1, 1), 0)
            self.hop(2, self.piece(3, 0), 1)
            self.rows(6, 2)

        def relay(self):
            for which in range(2):
                y_hops[self.s, which].wait_recv()
                part = self.piece((1, 3)[which], which)
                self.rx[6 + which] = (self.rx[which].astype(F32) + part[...].astype(F32)).astype(BF16)
                self.hop(4 + which, self.rx.at[6 + which], which)

        def total(self, which):
            y_hops[self.s, 2 + which].wait_recv()
            y_hops[self.s, 4 + which].wait_recv()
            part = self.piece(0, which)[...].astype(F32)
            return part + self.rx[2 + which].astype(F32) + self.rx[4 + which].astype(F32)

    stages = [Stage(s) for s in range(WHOLE + HALVES)]

    def finish(s):
        for which in range(2):
            total = stages[s].total(which)
            for jj in range(PAIR):
                tiles[which, PAIR * s + jj] = total[:, jj * tile:(jj + 1) * tile]

    def finish_halves(rank):
        s = WHOLE + 2 * rank
        j = blocks + 4 + 2 * rank
        for which in range(2):
            one, two = stages[s].total(which), stages[s + 1].total(which)
            low = lax.broadcasted_iota(jnp.int32, one.shape, 1) < tile // 2
            tiles[which, j] = jnp.where(low, one, pltpu.roll(two, tile // 2, 1))
            tiles[which, j + 1] = jnp.where(low, pltpu.roll(one, tile // 2, 1), two)

    forwards = {}

    def forward(rank):
        for side in range(2):
            hops[0, rank, side].wait_recv()
            k = 2 * rank + side
            copy = remote(far.at[0, k], far.at[1, k], fc_send.at[k], fc_recv.at[k], partner)
            copy.start()
            forwards[own_stages + rank, side] = copy

    def far_piece(slot, rank, half, side):
        return far.at[slot, 4 + 2 * rank + side, pl.ds(half * (ny // 2), ny // 2)]

    def forward_half(rank, half):
        for side in range(2):
            hops[2, rank, half, side].wait_recv()
            copy = remote(
                far_piece(0, rank, half, side), far_piece(1, rank, half, side),
                fb_send.at[rank, half, side], fb_recv.at[rank, half, side], partner,
            )
            copy.start()
            forwards[WHOLE + 2 * rank + half, side] = copy

    def pass_on(rank):
        for half in range(2):
            for side in range(2):
                if half == 0:
                    hops[1, rank, side].wait_recv()
                copy = remote(
                    relay.at[2 * rank + side, pl.ds(half * (ny // 2), ny // 2)], far_piece(0, rank, half, side),
                    b_send.at[rank, half, side], b_recv.at[rank, half, side], x_to[side],
                )
                copy.start()
                hops[2, rank, half, side] = copy

    def run_far(s):
        for side in range(2):
            forwards[s, side].wait_recv()
        stages[s].run()

    for s in range(own_stages):
        swaps[3 + s].wait_recv()
        stages[s].run()
    forward(0)
    stages[0].relay()
    stages[1].relay()
    run_far(4)
    stages[2].relay()
    pass_on(0)
    stages[3].relay()
    forward(1)
    stages[4].relay()
    run_far(5)
    finish(0)
    finish(1)
    finish(2)
    pass_on(1)
    finish(3)
    stages[5].relay()
    forward_half(0, 0)
    finish(4)
    run_far(6)
    forward_half(0, 1)
    run_far(7)
    finish(5)
    stages[6].relay()
    forward_half(1, 0)
    run_far(8)
    stages[7].relay()
    forward_half(1, 1)
    run_far(9)
    finish_halves(0)
    stages[8].relay()
    stages[9].relay()
    finish_halves(1)

    for copy in asks + swaps + list(hops.values()) + list(forwards.values()) + list(y_hops.values()):
        copy.wait_send()
    put_pos.wait()


def place_kernel(pos, tiles, density, energy):
    per, slots, keep, _ = density.shape
    first = pl.program_id(0) * per
    for i in range(per):
        rows = pl.ds(pl.multiple_of((first + i) * keep, keep), keep)
        for k in range(slots):
            p = pos[first + i, k]
            density[i, k] = tiles[0, p, rows, :]
            energy[i, k] = tiles[1, p, rows, :]


def body(eigvecs, occupations, energies, neighbours):
    bands = lax.axis_size("bands")
    blocks, slots = neighbours.shape
    rows, depth = eigvecs.shape
    tile = rows // blocks
    keep = tile // bands
    group = blocks * keep
    ny = bands // CORES
    wide = PAIR * tile
    block = (ny, CORES, keep, depth)
    any_space = pl.BlockSpec(memory_space=pl.ANY)
    dma = pltpu.SemaphoreType.DMA
    sems = []
    for shape in (
        (blocks // PAIR + 1,), (2,), (4,), (2, 2, 2), (2, 2, 2), (4,), (2, 2, 2), (WHOLE, 6), (HALVES, 6),
    ):
        sems += [dma(shape), dma(shape)]
    tiles, pos = pl.pallas_call(
        exchange_kernel,
        out_shape=(
            pltpu.VMEM((2, blocks + FAR, group, tile), F32),
            pltpu.SMEM((blocks, slots), jnp.int32),
        ),
        in_specs=[any_space] * 4,
        out_specs=(pl.BlockSpec(memory_space=pltpu.VMEM), pl.BlockSpec(memory_space=pltpu.SMEM)),
        scratch_shapes=[
            pltpu.VMEM((blocks, *block), BF16),
            pltpu.VMEM((blocks, *block), BF16),
            pltpu.VMEM((CORES, FAR, *block), BF16),
            pltpu.VMEM((CORES, ny * 2 * group, depth), BF16),
            pltpu.VMEM((CORES, 2, 1, depth), F32),
            pltpu.VMEM((WHOLE, ny * 2 * group, wide), BF16),
            pltpu.VMEM((WHOLE, 8, group, wide), BF16),
            pltpu.VMEM((HALVES, ny * 2 * group, wide // 2), BF16),
            pltpu.VMEM((HALVES, 8, group, wide // 2), BF16),
            pltpu.VMEM((FAR, *block), BF16),
            pltpu.VMEM((4, *block), BF16),
            pltpu.VMEM((4, 8, 128), jnp.int32),
            pltpu.VMEM((4, 8, 128), jnp.int32),
            pltpu.VMEM((blocks, slots), jnp.int32),
            pltpu.VMEM((blocks, slots), jnp.int32),
            dma((4,)),
            *sems,
            dma((1,)),
        ],
        compiler_params=pltpu.CompilerParams(
            collective_id=0, has_side_effects=True, vmem_limit_bytes=60 * 2**20
        ),
        name="exchange",
    )(
        eigvecs.reshape(blocks, *block), occupations.reshape(1, depth), energies.reshape(1, depth), neighbours
    )
    per = 4
    out = jax.ShapeDtypeStruct((blocks, slots, keep, tile), F32)
    density, energy = pl.pallas_call(
        place_kernel,
        out_shape=(out, out),
        grid=(blocks // per,),
        in_specs=[pl.BlockSpec(memory_space=pltpu.SMEM), pl.BlockSpec(memory_space=pltpu.VMEM)],
        out_specs=[pl.BlockSpec((per, slots, keep, tile), lambda i: (i, 0, 0, 0))] * 2,
        name="place",
    )(pos, pltpu.with_memory_space_constraint(tiles, pltpu.VMEM))
    return density, energy


def solution(mesh):
    return jax.shard_map(
        body,
        mesh=mesh,
        in_specs=(P("atoms", "bands"), P("bands"), P("bands"), P("atoms", None)),
        out_specs=(P("atoms", None, "bands", None), P("atoms", None, "bands", None)),
        check_vma=False,
    )
```

```python
import jax
import jax.numpy as jnp
from jax import lax
from jax.experimental import pallas as pl
from jax.experimental.pallas import tpu as pltpu
from jax.sharding import PartitionSpec as P

F32 = jnp.float32
BF16 = jnp.bfloat16
MESH = pl.DeviceIdType.MESH
CORES = 2
PAIR = 2
WHOLE = 6
HALVES = 4
FAR = 8
ORDER = (2, 1, 3, 0)


def exchange_kernel(
    eig, occ, en, neigh,
    tiles, pos_out,
    own, mate, far, lhs, vec,
    y_whole, rx_whole, y_half, rx_half,
    send, relay, req_out, req_in, neigh_v, pos_v,
    ld_sem, own_send, own_recv, vec_send, vec_recv, req_send, req_recv,
    x_send, x_recv, b_send, b_recv, fc_send, fc_recv, fb_send, fb_recv,
    yw_send, yw_recv, yh_send, yh_recv, out_sem,
):
    n = lax.axis_size("atoms")
    d = lax.axis_index("atoms")
    band = lax.axis_index("bands")
    y = band // CORES
    c = lax.rem(band, CORES)
    blocks, ny, _, keep, depth = eig.shape
    group = blocks * keep
    tile = ny * CORES * keep
    own_stages = blocks // PAIR

    def at_domain(step):
        return (lax.rem(d + step + n, n), band)

    def at_y(step):
        return (d, lax.rem(y + step + ny, ny) * CORES + c)

    partner = (d, y * CORES + 1 - c)
    x_to = (at_domain(1), at_domain(-1))
    y_to = (at_y(1), at_y(-1))
    peers = [at_domain(s) for s in (2, -2, 1, -1)] + [y_to[0], y_to[1], partner]

    barrier = pltpu.get_barrier_semaphore()
    for peer in peers:
        pl.semaphore_signal(barrier, inc=1, device_id=peer, device_id_type=MESH)

    load_ids = pltpu.make_async_copy(neigh, neigh_v, ld_sem.at[0])
    load_occ = pltpu.make_async_copy(occ, vec.at[0, 0], ld_sem.at[1])
    load_en = pltpu.make_async_copy(en, vec.at[0, 1], ld_sem.at[2])
    load_eig = pltpu.make_async_copy(eig, own, ld_sem.at[3])
    load_ids.start()
    load_eig.start()
    load_occ.start()
    load_en.start()

    load_ids.wait()
    ids = neigh_v[...]
    shift = blocks.bit_length() - 1
    owner = lax.shift_right_logical(ids, jnp.full_like(ids, shift))
    within = ids & (blocks - 1)
    row = lax.broadcasted_iota(jnp.int32, req_out.shape[1:], 0)
    steps = (-1, 1, -2, 2)
    masks, lows = [], []
    for q, step in enumerate(steps):
        mask = owner == lax.rem(d + step + n, n)
        low = jnp.min(jnp.where(mask, within, blocks - 1))
        high = jnp.max(jnp.where(mask, within, 0))
        req_out[q] = jnp.where(row == 0, low, high)
        masks.append(mask)
        lows.append(low)

    def remote(src, dst, s_sem, r_sem, to):
        return pltpu.make_async_remote_copy(
            src_ref=src, dst_ref=dst, send_sem=s_sem, recv_sem=r_sem,
            device_id=to, device_id_type=MESH,
        )

    pl.semaphore_wait(barrier, len(peers))

    asks = [
        remote(req_out.at[q], req_in.at[q], req_send.at[q], req_recv.at[q], at_domain(step))
        for q, step in enumerate(steps)
    ]
    swaps = [
        remote(occ, vec.at[1, 0], vec_send.at[0], vec_recv.at[0], partner),
        remote(en, vec.at[1, 1], vec_send.at[1], vec_recv.at[1], partner),
        remote(eig.at[:, :, 1 - c], mate.at[:, :, 1 - c], own_send.at[own_stages], own_recv.at[own_stages], partner),
    ]
    for s in range(own_stages):
        blk = pl.ds(s * PAIR, PAIR)
        swaps.append(remote(eig.at[blk, :, c], mate.at[blk, :, c], own_send.at[s], own_recv.at[s], partner))
    for copy in asks + swaps:
        copy.start()

    pos = within
    for q in range(4):
        base = blocks + 4 * (q // 2) + q % 2
        pos = jnp.where(masks[q], base + 2 * (within != lows[q]).astype(jnp.int32), pos)
    pos_v[...] = pos
    put_pos = pltpu.make_async_copy(pos_v, pos_out, out_sem.at[0])
    put_pos.start()

    def scale(kc, source):
        first = vec[kc, 0]
        second = first * vec[kc, 1]
        for k, rel in enumerate(ORDER):
            dest = lax.rem(y + rel, ny)

            def step(i, carry, k=k, dest=dest):
                x = source[i, dest, c].astype(F32)
                at = pl.multiple_of(2 * k * group + i * keep, keep)
                lhs[kc, pl.ds(at, keep), :] = (x * first).astype(BF16)
                at = pl.multiple_of((2 * k + 1) * group + i * keep, keep)
                lhs[kc, pl.ds(at, keep), :] = (x * second).astype(BF16)
                return carry

            lax.fori_loop(0, blocks, step, 0)

    load_occ.wait()
    load_en.wait()
    load_eig.wait()
    scale(0, own)

    hops = {}
    for rank in range(2):
        for kind in range(2):
            for side in range(2):
                q = 2 * kind + side
                if rank == 0:
                    asks[q].wait_recv()
                b = jnp.max(req_in[q, rank:rank + 1, :])
                send[2 * q + rank] = own[b]
            for side in range(2):
                q = 2 * kind + side
                dst = far.at[0, 2 * rank + side] if kind == 0 else relay.at[2 * rank + side]
                hops[kind, rank, side] = remote(
                    send.at[2 * q + rank], dst,
                    x_send.at[kind, rank, side], x_recv.at[kind, rank, side], x_to[side],
                )
                hops[kind, rank, side].start()

    for swap in swaps[:3]:
        swap.wait_recv()
    scale(1, mate)

    y_hops = {}
    dims = (((1,), (1,)), ((), ()))

    class Stage:
        def __init__(self, s):
            self.s = s
            if s < WHOLE:
                self.out, self.rx = y_whole.at[s], rx_whole.at[s]
                self.y_send, self.y_recv = yw_send.at[s], yw_recv.at[s]
            else:
                self.out, self.rx = y_half.at[s - WHOLE], rx_half.at[s - WHOLE]
                self.y_send, self.y_recv = yh_send.at[s - WHOLE], yh_recv.at[s - WHOLE]

        def right(self, k):
            s = self.s
            if s < own_stages:
                value = (own, mate)[k][pl.ds(s * PAIR, PAIR)]
            elif s < WHOLE:
                value = far[k, pl.ds((s - own_stages) * PAIR, PAIR)]
            else:
                rank, half = (s - WHOLE) // 2, (s - WHOLE) % 2
                value = far[k, pl.ds(4 + 2 * rank, PAIR), pl.ds(half * (ny // 2), ny // 2)]
            return value.reshape(-1, depth)

        def piece(self, rel, which):
            return self.out.at[pl.ds((2 * ORDER.index(rel) + which) * group, group), :]

        def rows(self, first, count):
            rows = pl.ds(first * group, count * group)
            total = lax.dot_general(lhs[0, rows, :], self.right(0), dims, preferred_element_type=F32)
            total += lax.dot_general(lhs[1, rows, :], self.right(1), dims, preferred_element_type=F32)
            self.out[rows, :] = total.astype(BF16)

        def hop(self, k, src, side):
            copy = remote(src, self.rx.at[k], self.y_send.at[k], self.y_recv.at[k], y_to[side])
            copy.start()
            y_hops[self.s, k] = copy

        def run(self):
            self.rows(0, 2)
            self.hop(0, self.piece(2, 0), 0)
            self.hop(1, self.piece(2, 1), 1)
            self.rows(2, 4)
            self.hop(3, self.piece(1, 1), 0)
            self.hop(2, self.piece(3, 0), 1)
            self.rows(6, 2)

        def relay(self):
            for which in range(2):
                y_hops[self.s, which].wait_recv()
                part = self.piece((1, 3)[which], which)
                self.rx[6 + which] = (self.rx[which].astype(F32) + part[...].astype(F32)).astype(BF16)
                self.hop(4 + which, self.rx.at[6 + which], which)

        def total(self, which):
            y_hops[self.s, 2 + which].wait_recv()
            y_hops[self.s, 4 + which].wait_recv()
            part = self.piece(0, which)[...].astype(F32)
            return part + self.rx[2 + which].astype(F32) + self.rx[4 + which].astype(F32)

    stages = [Stage(s) for s in range(WHOLE + HALVES)]

    def finish(s):
        for which in range(2):
            total = stages[s].total(which)
            for jj in range(PAIR):
                tiles[which, PAIR * s + jj] = total[:, jj * tile:(jj + 1) * tile]

    def finish_halves(rank):
        s = WHOLE + 2 * rank
        j = blocks + 4 + 2 * rank
        for which in range(2):
            one, two = stages[s].total(which), stages[s + 1].total(which)
            low = lax.broadcasted_iota(jnp.int32, one.shape, 1) < tile // 2
            tiles[which, j] = jnp.where(low, one, pltpu.roll(two, tile // 2, 1))
            tiles[which, j + 1] = jnp.where(low, pltpu.roll(one, tile // 2, 1), two)

    forwards = {}

    def forward(rank):
        for side in range(2):
            hops[0, rank, side].wait_recv()
            k = 2 * rank + side
            copy = remote(far.at[0, k], far.at[1, k], fc_send.at[k], fc_recv.at[k], partner)
            copy.start()
            forwards[own_stages + rank, side] = copy

    def far_piece(slot, rank, half, side):
        return far.at[slot, 4 + 2 * rank + side, pl.ds(half * (ny // 2), ny // 2)]

    def forward_half(rank, half):
        for side in range(2):
            hops[2, rank, half, side].wait_recv()
            copy = remote(
                far_piece(0, rank, half, side), far_piece(1, rank, half, side),
                fb_send.at[rank, half, side], fb_recv.at[rank, half, side], partner,
            )
            copy.start()
            forwards[WHOLE + 2 * rank + half, side] = copy

    def pass_on(rank):
        for half in range(2):
            for side in range(2):
                if half == 0:
                    hops[1, rank, side].wait_recv()
                copy = remote(
                    relay.at[2 * rank + side, pl.ds(half * (ny // 2), ny // 2)], far_piece(0, rank, half, side),
                    b_send.at[rank, half, side], b_recv.at[rank, half, side], x_to[side],
                )
                copy.start()
                hops[2, rank, half, side] = copy

    def run_far(s):
        for side in range(2):
            forwards[s, side].wait_recv()
        stages[s].run()

    for s in range(own_stages):
        swaps[3 + s].wait_recv()
        stages[s].run()
    forward(0)
    stages[0].relay()
    stages[1].relay()
    run_far(4)
    stages[2].relay()
    pass_on(0)
    stages[3].relay()
    forward(1)
    stages[4].relay()
    run_far(5)
    pass_on(1)
    finish(0)
    finish(1)
    finish(2)
    forward_half(0, 0)
    stages[5].relay()
    finish(3)
    finish(4)
    forward_half(0, 1)
    run_far(6)
    finish(5)
    forward_half(1, 0)
    run_far(7)
    stages[6].relay()
    forward_half(1, 1)
    run_far(8)
    stages[7].relay()
    run_far(9)
    finish_halves(0)
    stages[8].relay()
    stages[9].relay()
    finish_halves(1)

    for copy in asks + swaps + list(hops.values()) + list(forwards.values()) + list(y_hops.values()):
        copy.wait_send()
    put_pos.wait()


def place_kernel(pos, tiles, density, energy):
    per, slots, keep, _ = density.shape
    first = pl.program_id(0) * per
    for i in range(per):
        rows = pl.ds(pl.multiple_of((first + i) * keep, keep), keep)
        for k in range(slots):
            p = pos[first + i, k]
            density[i, k] = tiles[0, p, rows, :]
            energy[i, k] = tiles[1, p, rows, :]


def body(eigvecs, occupations, energies, neighbours):
    bands = lax.axis_size("bands")
    blocks, slots = neighbours.shape
    rows, depth = eigvecs.shape
    tile = rows // blocks
    keep = tile // bands
    group = blocks * keep
    ny = bands // CORES
    wide = PAIR * tile
    block = (ny, CORES, keep, depth)
    any_space = pl.BlockSpec(memory_space=pl.ANY)
    dma = pltpu.SemaphoreType.DMA
    sems = []
    for shape in (
        (blocks // PAIR + 1,), (2,), (4,), (2, 2, 2), (2, 2, 2), (4,), (2, 2, 2), (WHOLE, 6), (HALVES, 6),
    ):
        sems += [dma(shape), dma(shape)]
    tiles, pos = pl.pallas_call(
        exchange_kernel,
        out_shape=(
            pltpu.VMEM((2, blocks + FAR, group, tile), F32),
            pltpu.SMEM((blocks, slots), jnp.int32),
        ),
        in_specs=[any_space] * 4,
        out_specs=(pl.BlockSpec(memory_space=pltpu.VMEM), pl.BlockSpec(memory_space=pltpu.SMEM)),
        scratch_shapes=[
            pltpu.VMEM((blocks, *block), BF16),
            pltpu.VMEM((blocks, *block), BF16),
            pltpu.VMEM((CORES, FAR, *block), BF16),
            pltpu.VMEM((CORES, ny * 2 * group, depth), BF16),
            pltpu.VMEM((CORES, 2, 1, depth), F32),
            pltpu.VMEM((WHOLE, ny * 2 * group, wide), BF16),
            pltpu.VMEM((WHOLE, 8, group, wide), BF16),
            pltpu.VMEM((HALVES, ny * 2 * group, wide // 2), BF16),
            pltpu.VMEM((HALVES, 8, group, wide // 2), BF16),
            pltpu.VMEM((FAR, *block), BF16),
            pltpu.VMEM((4, *block), BF16),
            pltpu.VMEM((4, 8, 128), jnp.int32),
            pltpu.VMEM((4, 8, 128), jnp.int32),
            pltpu.VMEM((blocks, slots), jnp.int32),
            pltpu.VMEM((blocks, slots), jnp.int32),
            dma((4,)),
            *sems,
            dma((1,)),
        ],
        compiler_params=pltpu.CompilerParams(
            collective_id=0, has_side_effects=True, vmem_limit_bytes=60 * 2**20
        ),
        name="exchange",
    )(
        eigvecs.reshape(blocks, *block), occupations.reshape(1, depth), energies.reshape(1, depth), neighbours
    )
    per = 4
    out = jax.ShapeDtypeStruct((blocks, slots, keep, tile), F32)
    density, energy = pl.pallas_call(
        place_kernel,
        out_shape=(out, out),
        grid=(blocks // per,),
        in_specs=[pl.BlockSpec(memory_space=pltpu.SMEM), pl.BlockSpec(memory_space=pltpu.VMEM)],
        out_specs=[pl.BlockSpec((per, slots, keep, tile), lambda i: (i, 0, 0, 0))] * 2,
        name="place",
    )(pos, pltpu.with_memory_space_constraint(tiles, pltpu.VMEM))
    return density, energy


def solution(mesh):
    return jax.shard_map(
        body,
        mesh=mesh,
        in_specs=(P("atoms", "bands"), P("bands"), P("bands"), P("atoms", None)),
        out_specs=(P("atoms", None, "bands", None), P("atoms", None, "bands", None)),
        check_vma=False,
    )
```

```python
import jax
import jax.numpy as jnp
from jax import lax
from jax.experimental import pallas as pl
from jax.experimental.pallas import tpu as pltpu
from jax.sharding import PartitionSpec as P

F32 = jnp.float32
BF16 = jnp.bfloat16
MESH = pl.DeviceIdType.MESH
CORES = 2
PAIR = 2
WHOLE = 6
HALVES = 4
FAR = 8
ORDER = (2, 1, 3, 0)


def exchange_kernel(
    eig, occ, en, neigh,
    tiles, pos_out,
    own, mate, far, lhs, vec,
    y_whole, rx_whole, y_half, rx_half,
    send, relay, req_out, req_in, neigh_v, pos_v,
    ld_sem, own_send, own_recv, vec_send, vec_recv, req_send, req_recv,
    x_send, x_recv, b_send, b_recv, fc_send, fc_recv, fb_send, fb_recv,
    yw_send, yw_recv, yh_send, yh_recv, out_sem,
):
    n = lax.axis_size("atoms")
    d = lax.axis_index("atoms")
    band = lax.axis_index("bands")
    y = band // CORES
    c = lax.rem(band, CORES)
    blocks, ny, _, keep, depth = eig.shape
    group = blocks * keep
    tile = ny * CORES * keep
    own_stages = blocks // PAIR

    def at_domain(step):
        return (lax.rem(d + step + n, n), band)

    def at_y(step):
        return (d, lax.rem(y + step + ny, ny) * CORES + c)

    partner = (d, y * CORES + 1 - c)
    x_to = (at_domain(1), at_domain(-1))
    y_to = (at_y(1), at_y(-1))
    peers = [at_domain(s) for s in (2, -2, 1, -1)] + [y_to[0], y_to[1], partner]

    barrier = pltpu.get_barrier_semaphore()
    for peer in peers:
        pl.semaphore_signal(barrier, inc=1, device_id=peer, device_id_type=MESH)

    load_ids = pltpu.make_async_copy(neigh, neigh_v, ld_sem.at[0])
    load_occ = pltpu.make_async_copy(occ, vec.at[0, 0], ld_sem.at[1])
    load_en = pltpu.make_async_copy(en, vec.at[0, 1], ld_sem.at[2])
    load_eig = pltpu.make_async_copy(eig, own, ld_sem.at[3])
    load_ids.start()
    load_eig.start()
    load_occ.start()
    load_en.start()

    load_ids.wait()
    ids = neigh_v[...]
    shift = blocks.bit_length() - 1
    owner = lax.shift_right_logical(ids, jnp.full_like(ids, shift))
    within = ids & (blocks - 1)
    row = lax.broadcasted_iota(jnp.int32, req_out.shape[1:], 0)
    steps = (-1, 1, -2, 2)
    masks, lows = [], []
    for q, step in enumerate(steps):
        mask = owner == lax.rem(d + step + n, n)
        low = jnp.min(jnp.where(mask, within, blocks - 1))
        high = jnp.max(jnp.where(mask, within, 0))
        req_out[q] = jnp.where(row == 0, low, high)
        masks.append(mask)
        lows.append(low)

    def remote(src, dst, s_sem, r_sem, to):
        return pltpu.make_async_remote_copy(
            src_ref=src, dst_ref=dst, send_sem=s_sem, recv_sem=r_sem,
            device_id=to, device_id_type=MESH,
        )

    pl.semaphore_wait(barrier, len(peers))

    asks = [
        remote(req_out.at[q], req_in.at[q], req_send.at[q], req_recv.at[q], at_domain(step))
        for q, step in enumerate(steps)
    ]
    swaps = [
        remote(occ, vec.at[1, 0], vec_send.at[0], vec_recv.at[0], partner),
        remote(en, vec.at[1, 1], vec_send.at[1], vec_recv.at[1], partner),
        remote(eig.at[:, :, 1 - c], mate.at[:, :, 1 - c], own_send.at[own_stages], own_recv.at[own_stages], partner),
    ]
    for s in range(own_stages):
        blk = pl.ds(s * PAIR, PAIR)
        swaps.append(remote(eig.at[blk, :, c], mate.at[blk, :, c], own_send.at[s], own_recv.at[s], partner))
    for copy in asks + swaps:
        copy.start()

    pos = within
    for q in range(4):
        base = blocks + 4 * (q // 2) + q % 2
        pos = jnp.where(masks[q], base + 2 * (within != lows[q]).astype(jnp.int32), pos)
    pos_v[...] = pos
    put_pos = pltpu.make_async_copy(pos_v, pos_out, out_sem.at[0])
    put_pos.start()

    def scale(kc, source):
        first = vec[kc, 0]
        second = first * vec[kc, 1]
        for k, rel in enumerate(ORDER):
            dest = lax.rem(y + rel, ny)

            def step(i, carry, k=k, dest=dest):
                x = source[i, dest, c].astype(F32)
                at = pl.multiple_of(2 * k * group + i * keep, keep)
                lhs[kc, pl.ds(at, keep), :] = (x * first).astype(BF16)
                at = pl.multiple_of((2 * k + 1) * group + i * keep, keep)
                lhs[kc, pl.ds(at, keep), :] = (x * second).astype(BF16)
                return carry

            lax.fori_loop(0, blocks, step, 0)

    load_occ.wait()
    load_en.wait()
    load_eig.wait()
    scale(0, own)

    hops = {}
    for kind in range(2):
        for rank in range(2):
            for side in range(2):
                q = 2 * kind + side
                if rank == 0:
                    asks[q].wait_recv()
                b = jnp.max(req_in[q, rank:rank + 1, :])
                send[2 * q + rank] = own[b]
            for side in range(2):
                q = 2 * kind + side
                dst = far.at[0, 2 * rank + side] if kind == 0 else relay.at[2 * rank + side]
                hops[kind, rank, side] = remote(
                    send.at[2 * q + rank], dst,
                    x_send.at[kind, rank, side], x_recv.at[kind, rank, side], x_to[side],
                )
                hops[kind, rank, side].start()

    for swap in swaps[:3]:
        swap.wait_recv()
    scale(1, mate)

    y_hops = {}
    dims = (((1,), (1,)), ((), ()))

    class Stage:
        def __init__(self, s):
            self.s = s
            if s < WHOLE:
                self.out, self.rx = y_whole.at[s], rx_whole.at[s]
                self.y_send, self.y_recv = yw_send.at[s], yw_recv.at[s]
            else:
                self.out, self.rx = y_half.at[s - WHOLE], rx_half.at[s - WHOLE]
                self.y_send, self.y_recv = yh_send.at[s - WHOLE], yh_recv.at[s - WHOLE]

        def right(self, k):
            s = self.s
            if s < own_stages:
                value = (own, mate)[k][pl.ds(s * PAIR, PAIR)]
            elif s < WHOLE:
                value = far[k, pl.ds((s - own_stages) * PAIR, PAIR)]
            else:
                rank, half = (s - WHOLE) // 2, (s - WHOLE) % 2
                value = far[k, pl.ds(4 + 2 * rank, PAIR), pl.ds(half * (ny // 2), ny // 2)]
            return value.reshape(-1, depth)

        def piece(self, rel, which):
            return self.out.at[pl.ds((2 * ORDER.index(rel) + which) * group, group), :]

        def rows(self, first, count):
            rows = pl.ds(first * group, count * group)
            total = lax.dot_general(lhs[0, rows, :], self.right(0), dims, preferred_element_type=F32)
            total += lax.dot_general(lhs[1, rows, :], self.right(1), dims, preferred_element_type=F32)
            self.out[rows, :] = total.astype(BF16)

        def hop(self, k, src, side):
            copy = remote(src, self.rx.at[k], self.y_send.at[k], self.y_recv.at[k], y_to[side])
            copy.start()
            y_hops[self.s, k] = copy

        def run(self):
            self.rows(0, 2)
            self.hop(0, self.piece(2, 0), 0)
            self.hop(1, self.piece(2, 1), 1)
            self.rows(2, 4)
            self.hop(3, self.piece(1, 1), 0)
            self.hop(2, self.piece(3, 0), 1)
            if self.s < WHOLE:
                self.rows(6, 2)

        def relay(self):
            for which in range(2):
                y_hops[self.s, which].wait_recv()
                part = self.piece((1, 3)[which], which)
                self.rx[6 + which] = (self.rx[which].astype(F32) + part[...].astype(F32)).astype(BF16)
                self.hop(4 + which, self.rx.at[6 + which], which)

        def total(self, which):
            y_hops[self.s, 2 + which].wait_recv()
            y_hops[self.s, 4 + which].wait_recv()
            part = self.piece(0, which)[...].astype(F32)
            return part + self.rx[2 + which].astype(F32) + self.rx[4 + which].astype(F32)

    stages = [Stage(s) for s in range(WHOLE + HALVES)]

    def finish(s):
        for which in range(2):
            total = stages[s].total(which)
            for jj in range(PAIR):
                tiles[which, PAIR * s + jj] = total[:, jj * tile:(jj + 1) * tile]

    def finish_halves(rank):
        s = WHOLE + 2 * rank
        j = blocks + 4 + 2 * rank
        for which in range(2):
            one, two = stages[s].total(which), stages[s + 1].total(which)
            low = lax.broadcasted_iota(jnp.int32, one.shape, 1) < tile // 2
            tiles[which, j] = jnp.where(low, one, pltpu.roll(two, tile // 2, 1))
            tiles[which, j + 1] = jnp.where(low, pltpu.roll(one, tile // 2, 1), two)

    forwards = {}

    def forward(rank):
        for side in range(2):
            hops[0, rank, side].wait_recv()
            k = 2 * rank + side
            copy = remote(far.at[0, k], far.at[1, k], fc_send.at[k], fc_recv.at[k], partner)
            copy.start()
            forwards[own_stages + rank, side] = copy

    def far_piece(slot, rank, half, side):
        return far.at[slot, 4 + 2 * rank + side, pl.ds(half * (ny // 2), ny // 2)]

    def forward_half(rank, half):
        for side in range(2):
            hops[2, rank, half, side].wait_recv()
            copy = remote(
                far_piece(0, rank, half, side), far_piece(1, rank, half, side),
                fb_send.at[rank, half, side], fb_recv.at[rank, half, side], partner,
            )
            copy.start()
            forwards[WHOLE + 2 * rank + half, side] = copy

    def pass_on(rank):
        for half in range(2):
            for side in range(2):
                if half == 0:
                    hops[1, rank, side].wait_recv()
                copy = remote(
                    relay.at[2 * rank + side, pl.ds(half * (ny // 2), ny // 2)], far_piece(0, rank, half, side),
                    b_send.at[rank, half, side], b_recv.at[rank, half, side], x_to[side],
                )
                copy.start()
                hops[2, rank, half, side] = copy

    def run_far(s):
        for side in range(2):
            forwards[s, side].wait_recv()
        stages[s].run()

    for s in range(own_stages):
        swaps[3 + s].wait_recv()
        stages[s].run()
    forward(0)
    stages[0].relay()
    stages[1].relay()
    run_far(4)
    forward(1)
    stages[2].relay()
    stages[3].relay()
    run_far(5)
    pass_on(0)
    finish(0)
    finish(1)
    stages[4].relay()
    finish(2)
    pass_on(1)
    forward_half(0, 0)
    stages[5].relay()
    finish(3)
    finish(4)
    forward_half(0, 1)
    run_far(6)
    finish(5)
    forward_half(1, 0)
    run_far(7)
    stages[6].relay()
    forward_half(1, 1)
    run_far(8)
    stages[7].relay()
    run_far(9)
    for s in range(WHOLE, WHOLE + HALVES):
        stages[s].rows(6, 2)
    stages[8].relay()
    finish_halves(0)
    stages[9].relay()
    finish_halves(1)

    for copy in asks + swaps + list(hops.values()) + list(forwards.values()) + list(y_hops.values()):
        copy.wait_send()
    put_pos.wait()


def place_kernel(pos, tiles, density, energy):
    per, slots, keep, _ = density.shape
    first = pl.program_id(0) * per
    for i in range(per):
        rows = pl.ds(pl.multiple_of((first + i) * keep, keep), keep)
        for k in range(slots):
            p = pos[first + i, k]
            density[i, k] = tiles[0, p, rows, :]
            energy[i, k] = tiles[1, p, rows, :]


def body(eigvecs, occupations, energies, neighbours):
    bands = lax.axis_size("bands")
    blocks, slots = neighbours.shape
    rows, depth = eigvecs.shape
    tile = rows // blocks
    keep = tile // bands
    group = blocks * keep
    ny = bands // CORES
    wide = PAIR * tile
    block = (ny, CORES, keep, depth)
    any_space = pl.BlockSpec(memory_space=pl.ANY)
    dma = pltpu.SemaphoreType.DMA
    sems = []
    for shape in (
        (blocks // PAIR + 1,), (2,), (4,), (2, 2, 2), (2, 2, 2), (4,), (2, 2, 2), (WHOLE, 6), (HALVES, 6),
    ):
        sems += [dma(shape), dma(shape)]
    tiles, pos = pl.pallas_call(
        exchange_kernel,
        out_shape=(
            pltpu.VMEM((2, blocks + FAR, group, tile), F32),
            pltpu.SMEM((blocks, slots), jnp.int32),
        ),
        in_specs=[any_space] * 4,
        out_specs=(pl.BlockSpec(memory_space=pltpu.VMEM), pl.BlockSpec(memory_space=pltpu.SMEM)),
        scratch_shapes=[
            pltpu.VMEM((blocks, *block), BF16),
            pltpu.VMEM((blocks, *block), BF16),
            pltpu.VMEM((CORES, FAR, *block), BF16),
            pltpu.VMEM((CORES, ny * 2 * group, depth), BF16),
            pltpu.VMEM((CORES, 2, 1, depth), F32),
            pltpu.VMEM((WHOLE, ny * 2 * group, wide), BF16),
            pltpu.VMEM((WHOLE, 8, group, wide), BF16),
            pltpu.VMEM((HALVES, ny * 2 * group, wide // 2), BF16),
            pltpu.VMEM((HALVES, 8, group, wide // 2), BF16),
            pltpu.VMEM((FAR, *block), BF16),
            pltpu.VMEM((4, *block), BF16),
            pltpu.VMEM((4, 8, 128), jnp.int32),
            pltpu.VMEM((4, 8, 128), jnp.int32),
            pltpu.VMEM((blocks, slots), jnp.int32),
            pltpu.VMEM((blocks, slots), jnp.int32),
            dma((4,)),
            *sems,
            dma((1,)),
        ],
        compiler_params=pltpu.CompilerParams(
            collective_id=0, has_side_effects=True, vmem_limit_bytes=60 * 2**20
        ),
        name="exchange",
    )(
        eigvecs.reshape(blocks, *block), occupations.reshape(1, depth), energies.reshape(1, depth), neighbours
    )
    per = 4
    out = jax.ShapeDtypeStruct((blocks, slots, keep, tile), F32)
    density, energy = pl.pallas_call(
        place_kernel,
        out_shape=(out, out),
        grid=(blocks // per,),
        in_specs=[pl.BlockSpec(memory_space=pltpu.SMEM), pl.BlockSpec(memory_space=pltpu.VMEM)],
        out_specs=[pl.BlockSpec((per, slots, keep, tile), lambda i: (i, 0, 0, 0))] * 2,
        name="place",
    )(pos, pltpu.with_memory_space_constraint(tiles, pltpu.VMEM))
    return density, energy


def solution(mesh):
    return jax.shard_map(
        body,
        mesh=mesh,
        in_specs=(P("atoms", "bands"), P("bands"), P("bands"), P("atoms", None)),
        out_specs=(P("atoms", None, "bands", None), P("atoms", None, "bands", None)),
        check_vma=False,
    )
```

```python
import jax
import jax.numpy as jnp
from jax import lax
from jax.experimental import pallas as pl
from jax.experimental.pallas import tpu as pltpu
from jax.sharding import PartitionSpec as P

F32 = jnp.float32
BF16 = jnp.bfloat16
MESH = pl.DeviceIdType.MESH
CORES = 2
PAIR = 2
WHOLE = 6
HALVES = 4
FAR = 8
ORDER = (2, 1, 3, 0)


def exchange_kernel(
    eig, occ, en, neigh,
    tiles, pos_out,
    own, mate, far, lhs, vec,
    y_whole, rx_whole, y_half, rx_half,
    send, relay, req_out, req_in, neigh_v, pos_v,
    ld_sem, own_send, own_recv, vec_send, vec_recv, req_send, req_recv,
    x_send, x_recv, b_send, b_recv, fc_send, fc_recv, fb_send, fb_recv,
    yw_send, yw_recv, yh_send, yh_recv, out_sem,
):
    n = lax.axis_size("atoms")
    d = lax.axis_index("atoms")
    band = lax.axis_index("bands")
    y = band // CORES
    c = lax.rem(band, CORES)
    blocks, ny, _, keep, depth = eig.shape
    group = blocks * keep
    tile = ny * CORES * keep
    own_stages = blocks // PAIR

    def at_domain(step):
        return (lax.rem(d + step + n, n), band)

    def at_y(step):
        return (d, lax.rem(y + step + ny, ny) * CORES + c)

    partner = (d, y * CORES + 1 - c)
    x_to = (at_domain(1), at_domain(-1))
    y_to = (at_y(1), at_y(-1))
    peers = [at_domain(s) for s in (2, -2, 1, -1)] + [y_to[0], y_to[1], partner]

    barrier = pltpu.get_barrier_semaphore()
    for peer in peers:
        pl.semaphore_signal(barrier, inc=1, device_id=peer, device_id_type=MESH)

    load_ids = pltpu.make_async_copy(neigh, neigh_v, ld_sem.at[0])
    load_occ = pltpu.make_async_copy(occ, vec.at[0, 0], ld_sem.at[1])
    load_en = pltpu.make_async_copy(en, vec.at[0, 1], ld_sem.at[2])
    load_eig = pltpu.make_async_copy(eig, own, ld_sem.at[3])
    load_ids.start()
    load_eig.start()
    load_occ.start()
    load_en.start()

    load_ids.wait()
    ids = neigh_v[...]
    shift = blocks.bit_length() - 1
    owner = lax.shift_right_logical(ids, jnp.full_like(ids, shift))
    within = ids & (blocks - 1)
    row = lax.broadcasted_iota(jnp.int32, req_out.shape[1:], 0)
    steps = (-1, 1, -2, 2)
    masks, lows = [], []
    for q, step in enumerate(steps):
        mask = owner == lax.rem(d + step + n, n)
        low = jnp.min(jnp.where(mask, within, blocks - 1))
        high = jnp.max(jnp.where(mask, within, 0))
        req_out[q] = jnp.where(row == 0, low, high)
        masks.append(mask)
        lows.append(low)

    def remote(src, dst, s_sem, r_sem, to):
        return pltpu.make_async_remote_copy(
            src_ref=src, dst_ref=dst, send_sem=s_sem, recv_sem=r_sem,
            device_id=to, device_id_type=MESH,
        )

    pl.semaphore_wait(barrier, len(peers))

    asks = [
        remote(req_out.at[q], req_in.at[q], req_send.at[q], req_recv.at[q], at_domain(step))
        for q, step in enumerate(steps)
    ]
    swaps = [
        remote(occ, vec.at[1, 0], vec_send.at[0], vec_recv.at[0], partner),
        remote(en, vec.at[1, 1], vec_send.at[1], vec_recv.at[1], partner),
        remote(eig.at[:, :, 1 - c], mate.at[:, :, 1 - c], own_send.at[own_stages], own_recv.at[own_stages], partner),
    ]
    for s in range(own_stages):
        blk = pl.ds(s * PAIR, PAIR)
        swaps.append(remote(eig.at[blk, :, c], mate.at[blk, :, c], own_send.at[s], own_recv.at[s], partner))
    for copy in asks + swaps:
        copy.start()

    pos = within
    for q in range(4):
        base = blocks + 4 * (q // 2) + q % 2
        pos = jnp.where(masks[q], base + 2 * (within != lows[q]).astype(jnp.int32), pos)
    pos_v[...] = pos
    put_pos = pltpu.make_async_copy(pos_v, pos_out, out_sem.at[0])
    put_pos.start()

    def scale(kc, source):
        first = vec[kc, 0]
        second = first * vec[kc, 1]
        for k, rel in enumerate(ORDER):
            dest = lax.rem(y + rel, ny)

            def step(i, carry, k=k, dest=dest):
                x = source[i, dest, c].astype(F32)
                at = pl.multiple_of(2 * k * group + i * keep, keep)
                lhs[kc, pl.ds(at, keep), :] = (x * first).astype(BF16)
                at = pl.multiple_of((2 * k + 1) * group + i * keep, keep)
                lhs[kc, pl.ds(at, keep), :] = (x * second).astype(BF16)
                return carry

            lax.fori_loop(0, blocks, step, 0)

    load_occ.wait()
    load_en.wait()
    load_eig.wait()
    scale(0, own)

    hops = {}
    def leave(kind):
        for rank in range(2):
            for side in range(2):
                q = 2 * kind + side
                if rank == 0:
                    asks[q].wait_recv()
                b = jnp.max(req_in[q, rank:rank + 1, :])
                send[2 * q + rank] = own[b]
            for side in range(2):
                q = 2 * kind + side
                dst = far.at[0, 2 * rank + side] if kind == 0 else relay.at[2 * rank + side]
                hops[kind, rank, side] = remote(
                    send.at[2 * q + rank], dst,
                    x_send.at[kind, rank, side], x_recv.at[kind, rank, side], x_to[side],
                )
                hops[kind, rank, side].start()

    leave(0)
    for swap in swaps[:3]:
        swap.wait_recv()
    scale(1, mate)

    y_hops = {}
    dims = (((1,), (1,)), ((), ()))

    class Stage:
        def __init__(self, s):
            self.s = s
            if s < WHOLE:
                self.out, self.rx = y_whole.at[s], rx_whole.at[s]
                self.y_send, self.y_recv = yw_send.at[s], yw_recv.at[s]
            else:
                self.out, self.rx = y_half.at[s - WHOLE], rx_half.at[s - WHOLE]
                self.y_send, self.y_recv = yh_send.at[s - WHOLE], yh_recv.at[s - WHOLE]

        def right(self, k):
            s = self.s
            if s < own_stages:
                value = (own, mate)[k][pl.ds(s * PAIR, PAIR)]
            elif s < WHOLE:
                value = far[k, pl.ds((s - own_stages) * PAIR, PAIR)]
            else:
                rank, half = (s - WHOLE) // 2, (s - WHOLE) % 2
                value = far[k, pl.ds(4 + 2 * rank, PAIR), pl.ds(half * (ny // 2), ny // 2)]
            return value.reshape(-1, depth)

        def piece(self, rel, which):
            return self.out.at[pl.ds((2 * ORDER.index(rel) + which) * group, group), :]

        def rows(self, first, count):
            rows = pl.ds(first * group, count * group)
            total = lax.dot_general(lhs[0, rows, :], self.right(0), dims, preferred_element_type=F32)
            total += lax.dot_general(lhs[1, rows, :], self.right(1), dims, preferred_element_type=F32)
            self.out[rows, :] = total.astype(BF16)

        def hop(self, k, src, side):
            copy = remote(src, self.rx.at[k], self.y_send.at[k], self.y_recv.at[k], y_to[side])
            copy.start()
            y_hops[self.s, k] = copy

        def run(self):
            self.rows(0, 2)
            self.hop(0, self.piece(2, 0), 0)
            self.hop(1, self.piece(2, 1), 1)
            self.rows(2, 4)
            self.hop(3, self.piece(1, 1), 0)
            self.hop(2, self.piece(3, 0), 1)
            if self.s < WHOLE:
                self.rows(6, 2)

        def relay(self):
            for which in range(2):
                y_hops[self.s, which].wait_recv()
                part = self.piece((1, 3)[which], which)
                self.rx[6 + which] = (self.rx[which].astype(F32) + part[...].astype(F32)).astype(BF16)
                self.hop(4 + which, self.rx.at[6 + which], which)

        def total(self, which):
            y_hops[self.s, 2 + which].wait_recv()
            y_hops[self.s, 4 + which].wait_recv()
            part = self.piece(0, which)[...].astype(F32)
            return part + self.rx[2 + which].astype(F32) + self.rx[4 + which].astype(F32)

    stages = [Stage(s) for s in range(WHOLE + HALVES)]

    def finish(s):
        for which in range(2):
            total = stages[s].total(which)
            for jj in range(PAIR):
                tiles[which, PAIR * s + jj] = total[:, jj * tile:(jj + 1) * tile]

    def finish_halves(rank):
        s = WHOLE + 2 * rank
        j = blocks + 4 + 2 * rank
        for which in range(2):
            one, two = stages[s].total(which), stages[s + 1].total(which)
            low = lax.broadcasted_iota(jnp.int32, one.shape, 1) < tile // 2
            tiles[which, j] = jnp.where(low, one, pltpu.roll(two, tile // 2, 1))
            tiles[which, j + 1] = jnp.where(low, pltpu.roll(one, tile // 2, 1), two)

    forwards = {}

    def forward(rank):
        for side in range(2):
            hops[0, rank, side].wait_recv()
            k = 2 * rank + side
            copy = remote(far.at[0, k], far.at[1, k], fc_send.at[k], fc_recv.at[k], partner)
            copy.start()
            forwards[own_stages + rank, side] = copy

    def far_piece(slot, rank, half, side):
        return far.at[slot, 4 + 2 * rank + side, pl.ds(half * (ny // 2), ny // 2)]

    def forward_half(rank, half):
        for side in range(2):
            hops[2, rank, half, side].wait_recv()
            copy = remote(
                far_piece(0, rank, half, side), far_piece(1, rank, half, side),
                fb_send.at[rank, half, side], fb_recv.at[rank, half, side], partner,
            )
            copy.start()
            forwards[WHOLE + 2 * rank + half, side] = copy

    def pass_on(rank):
        for half in range(2):
            for side in range(2):
                if half == 0:
                    hops[1, rank, side].wait_recv()
                copy = remote(
                    relay.at[2 * rank + side, pl.ds(half * (ny // 2), ny // 2)], far_piece(0, rank, half, side),
                    b_send.at[rank, half, side], b_recv.at[rank, half, side], x_to[side],
                )
                copy.start()
                hops[2, rank, half, side] = copy

    def run_far(s):
        for side in range(2):
            forwards[s, side].wait_recv()
        stages[s].run()

    swaps[3].wait_recv()
    stages[0].run()
    leave(1)
    for s in range(1, own_stages):
        swaps[3 + s].wait_recv()
        stages[s].run()
    forward(0)
    stages[0].relay()
    stages[1].relay()
    run_far(4)
    forward(1)
    stages[2].relay()
    stages[3].relay()
    run_far(5)
    pass_on(0)
    finish(0)
    finish(1)
    stages[4].relay()
    finish(2)
    pass_on(1)
    forward_half(0, 0)
    stages[5].relay()
    finish(3)
    finish(4)
    forward_half(0, 1)
    run_far(6)
    forward_half(1, 0)
    run_far(7)
    stages[6].relay()
    forward_half(1, 1)
    run_far(8)
    stages[7].relay()
    run_far(9)
    stages[8].relay()
    for s in range(WHOLE, WHOLE + HALVES):
        stages[s].rows(6, 2)
    stages[9].relay()
    finish(5)
    finish_halves(0)
    finish_halves(1)

    for copy in asks + swaps + list(hops.values()) + list(forwards.values()) + list(y_hops.values()):
        copy.wait_send()
    put_pos.wait()


def place_kernel(pos, tiles, density, energy):
    per, slots, keep, _ = density.shape
    first = pl.program_id(0) * per
    for i in range(per):
        rows = pl.ds(pl.multiple_of((first + i) * keep, keep), keep)
        for k in range(slots):
            p = pos[first + i, k]
            density[i, k] = tiles[0, p, rows, :]
            energy[i, k] = tiles[1, p, rows, :]


def body(eigvecs, occupations, energies, neighbours):
    bands = lax.axis_size("bands")
    blocks, slots = neighbours.shape
    rows, depth = eigvecs.shape
    tile = rows // blocks
    keep = tile // bands
    group = blocks * keep
    ny = bands // CORES
    wide = PAIR * tile
    block = (ny, CORES, keep, depth)
    any_space = pl.BlockSpec(memory_space=pl.ANY)
    dma = pltpu.SemaphoreType.DMA
    sems = []
    for shape in (
        (blocks // PAIR + 1,), (2,), (4,), (2, 2, 2), (2, 2, 2), (4,), (2, 2, 2), (WHOLE, 6), (HALVES, 6),
    ):
        sems += [dma(shape), dma(shape)]
    tiles, pos = pl.pallas_call(
        exchange_kernel,
        out_shape=(
            pltpu.VMEM((2, blocks + FAR, group, tile), F32),
            pltpu.SMEM((blocks, slots), jnp.int32),
        ),
        in_specs=[any_space] * 4,
        out_specs=(pl.BlockSpec(memory_space=pltpu.VMEM), pl.BlockSpec(memory_space=pltpu.SMEM)),
        scratch_shapes=[
            pltpu.VMEM((blocks, *block), BF16),
            pltpu.VMEM((blocks, *block), BF16),
            pltpu.VMEM((CORES, FAR, *block), BF16),
            pltpu.VMEM((CORES, ny * 2 * group, depth), BF16),
            pltpu.VMEM((CORES, 2, 1, depth), F32),
            pltpu.VMEM((WHOLE, ny * 2 * group, wide), BF16),
            pltpu.VMEM((WHOLE, 8, group, wide), BF16),
            pltpu.VMEM((HALVES, ny * 2 * group, wide // 2), BF16),
            pltpu.VMEM((HALVES, 8, group, wide // 2), BF16),
            pltpu.VMEM((FAR, *block), BF16),
            pltpu.VMEM((4, *block), BF16),
            pltpu.VMEM((4, 8, 128), jnp.int32),
            pltpu.VMEM((4, 8, 128), jnp.int32),
            pltpu.VMEM((blocks, slots), jnp.int32),
            pltpu.VMEM((blocks, slots), jnp.int32),
            dma((4,)),
            *sems,
            dma((1,)),
        ],
        compiler_params=pltpu.CompilerParams(
            collective_id=0, has_side_effects=True, vmem_limit_bytes=60 * 2**20
        ),
        name="exchange",
    )(
        eigvecs.reshape(blocks, *block), occupations.reshape(1, depth), energies.reshape(1, depth), neighbours
    )
    per = 4
    out = jax.ShapeDtypeStruct((blocks, slots, keep, tile), F32)
    density, energy = pl.pallas_call(
        place_kernel,
        out_shape=(out, out),
        grid=(blocks // per,),
        in_specs=[pl.BlockSpec(memory_space=pltpu.SMEM), pl.BlockSpec(memory_space=pltpu.VMEM)],
        out_specs=[pl.BlockSpec((per, slots, keep, tile), lambda i: (i, 0, 0, 0))] * 2,
        name="place",
    )(pos, pltpu.with_memory_space_constraint(tiles, pltpu.VMEM))
    return density, energy


def solution(mesh):
    return jax.shard_map(
        body,
        mesh=mesh,
        in_specs=(P("atoms", "bands"), P("bands"), P("bands"), P("atoms", None)),
        out_specs=(P("atoms", None, "bands", None), P("atoms", None, "bands", None)),
        check_vma=False,
    )
```
